32 devices in a mesh: row: 8 (over z, y), col: 4 (over x, core).
Axes of the slice: x: 2, y: 2, z: 4, core: 2. Of those that a mesh axis runs over, the one named last changes fastest.
Arguments:
- upper: bfloat16 [4096, 8, 4, 128], P('row', None, 'col'), as said below
- signs: int32 [4096, 512], P(('row', 'col')), may hold values from 0 to 1
- weights: float32 [4096], P(('row', 'col')), may hold values from 0.5 to 2
- components: float32 [2], replicated, may hold values from 0.3 to 3
Outputs:
- applied: float32 [4096, 512], P(('row', 'col'))
The draws below stay inside these ranges and needn't reach their ends.
Inputs may be any that keep to these rules, and one draw needn't show every extreme that they name: upper's first dimension and its flattened column index count the same samples in the same order.
All inputs are finite; a program needn't handle non-finite values.
Results may differ from the reference program's by a relative error of at most 0.0055.
Values may be sent and summed in bfloat16 or wider, within the bound.
No kernel may reach another device: no remote copies, remote signals or barrier semaphores. Data moves between devices by JAX's collectives and lax.ppermute only.
A program may use at most 128 MiB of HBM per device.

```python
import math
import jax
import jax.numpy as jnp
from jax import lax

FINE = 128
PROBES = 512
NTILES = 8
TILE = 512
SAMPLES = 4096
N_COL = 4


def draw_upper(key, part):
    shape = (SAMPLES, NTILES, N_COL, FINE)
    rowpos = lax.broadcasted_iota(jnp.int32, shape, 0)
    colpos = lax.broadcasted_iota(jnp.int32, shape, 1) * (N_COL * FINE) + lax.broadcasted_iota(jnp.int32, shape, 2) * FINE + lax.broadcasted_iota(jnp.int32, shape, 3)
    noise = jax.random.normal(key, shape, jnp.float32)
    values = 0.5 * noise * SAMPLES ** (-0.5) + jnp.where(rowpos == colpos, 1.0, 0.0)
    return values.astype(jnp.bfloat16)


def place_ends(drawn, stream_key, least, top_value):
    index_at = [jax.random.randint(jax.random.fold_in(stream_key, axis), (), 0, length) for axis, length in enumerate(drawn.shape)]
    longest = drawn.shape.index(max(drawn.shape))
    neighbour = index_at[:longest] + [(index_at[longest] + 1) % drawn.shape[longest]] + index_at[longest + 1:]
    return drawn.at[tuple(index_at)].set(least).at[tuple(neighbour)].set(top_value)


def block_scale(rng, extent, split, low, high):
    loudness, own = 1.0, jax.random.fold_in(rng, 6)
    for axis_at, blocks in split:
        draws = jnp.exp(jax.random.uniform(jax.random.fold_in(own, axis_at), (blocks,), jnp.float32, low / len(split), high / len(split)))
        loudness = loudness * jnp.repeat(draws, extent[axis_at] // blocks).reshape([-1 if axis == axis_at else 1 for axis in range(len(extent))])
    return loudness


def setup_inputs(seed: int = 0) -> dict:
    seeds = jax.random.split(jax.random.key(seed), 5)
    return {
        "upper": draw_upper(jax.random.fold_in(seeds[4], 71), 0),
        "signs": place_ends(jax.random.randint(seeds[1], (SAMPLES, PROBES), 0, 2), jax.random.fold_in(seeds[1], 1), 0, 1).astype(jnp.int32),
        "weights": jnp.clip(jnp.exp(math.log(2.0) - 1.3862944 * jax.random.uniform(seeds[2], (SAMPLES,), jnp.float32) ** block_scale(seeds[2], (SAMPLES,), ((0, 32),), -0.2, 0.2)), 0.5, 2.0),
        "components": jnp.clip(jnp.exp(jax.random.uniform(seeds[3], (2,), jnp.float32, math.log(0.3), math.log(3.0))), 0.3, 3.0),
    }


def reference(upper, signs, weights, components):
    flat = upper.reshape(SAMPLES, SAMPLES)
    probes = ((2 * signs - 1).astype(jnp.float32) * weights[:, None]).astype(jnp.bfloat16)

    def tile_row(total, index):
        start = index * TILE
        block = lax.dynamic_slice_in_dim(flat, start, TILE, 0)
        rowpos = start + lax.broadcasted_iota(jnp.int32, (TILE, SAMPLES), 0)
        colpos = lax.broadcasted_iota(jnp.int32, (TILE, SAMPLES), 1)
        zero = jnp.zeros((), jnp.bfloat16)
        keep_up = jnp.where(colpos >= rowpos, block, zero)
        keep_strict = jnp.where(colpos > rowpos, block, zero)
        own = lax.dynamic_slice_in_dim(probes, start, TILE, 0)
        direct = jnp.dot(keep_up, probes, preferred_element_type=jnp.float32)
        mirror = jnp.dot(keep_strict.T, own, preferred_element_type=jnp.float32)
        total = total + mirror
        total = lax.dynamic_update_slice_in_dim(total, lax.dynamic_slice_in_dim(total, start, TILE, 0) + direct, start, 0)
        return total, None

    start_total = jnp.zeros((SAMPLES, PROBES), jnp.float32)
    product, _ = lax.scan(tile_row, start_total, jnp.arange(NTILES, dtype=jnp.int32))
    return components[0] * product + components[1] * probes.astype(jnp.float32)
```

```python
import jax
import jax.numpy as jnp
from jax import lax
from jax.sharding import PartitionSpec as P


def solution(mesh):
    nrow, ncol = mesh.shape["row"], mesh.shape["col"]
    ny, nk = 2, 2
    nz, nx = nrow // ny, ncol // nk
    both = ("row", "col")

    def place(z, y, x, k):
        return ((z * ny + y) * nx + x) * nk + k

    spots = [(z, y, x, k) for z in range(nz) for y in range(ny) for x in range(nx) for k in range(nk)]

    def down(d):
        return [(place(z, y, x, k), place(z - d, y, x, k)) for z, y, x, k in spots if z >= d]

    def up(d):
        return [(place(z, y, x, k), place(z + d, y, x, k)) for z, y, x, k in spots if z + d < nz]

    def shift(s, e):
        return [(place(z, y, x, k), place(z, y ^ s, (x + e) % nx, k)) for z, y, x, k in spots]

    other_core = [(place(z, y, x, k), place(z, y, x, 1 - k)) for z, y, x, k in spots]
    away = [(s, e) for s in range(ny) for e in range(nx) if (s, e) != (0, 0)]

    def body(upper, signs, weights, components):
        rows, ntiles, _, fine = upper.shape
        npro = signs.shape[1]
        r, c = lax.axis_index("row"), lax.axis_index("col")
        z, y, x, k = r // ny, r % ny, c // nk, c % nk
        f32, bf16 = jnp.float32, jnp.bfloat16
        probes = ((2 * signs - 1).astype(f32) * weights[:, None]).astype(bf16)
        flat = upper.reshape(rows, ntiles * fine)

        def column(d, side):
            tile = ((z + d) % nz) * ny + side
            return lax.dynamic_slice_in_dim(flat, tile * fine, fine, 1)

        rowpos = lax.broadcasted_iota(jnp.int32, (rows, fine), 0)
        colpos = c * fine + lax.broadcasted_iota(jnp.int32, (rows, fine), 1)
        zero = jnp.zeros((), bf16)
        diag_block = column(0, y)
        own = jnp.concatenate(
            [jnp.where(colpos > rowpos, diag_block, zero)] + [column(d, y) for d in range(1, nz)], axis=1
        )
        give = jnp.concatenate(
            [jnp.where(y == 0, column(0, 1 - y), zero)] + [column(d, 1 - y) for d in range(1, nz)], axis=1
        )
        oth = lax.ppermute(give, both, shift(1, 0))
        diag = jnp.sum(jnp.where(colpos == rowpos, diag_block.astype(f32), 0.0), axis=0)

        mine = {(0, 0): probes}
        for s, e in away:
            mine[s, e] = lax.ppermute(probes, both, shift(s, (nx - e) % nx))
        pcat = jnp.concatenate([probes] + [lax.ppermute(probes, both, down(d)) for d in range(1, nz)], axis=0)

        stack = jnp.stack([jnp.stack([mine[s, e] for e in range(nx)]) for s in range(ny)])
        got = lax.ppermute(stack, both, other_core)
        pair = jnp.where(k == 0, jnp.stack([stack, got], axis=2), jnp.stack([got, stack], axis=2))
        pair = lax.dynamic_slice_in_dim(jnp.concatenate([pair, pair], axis=1), (nx - x) % nx, nx, 1)
        q_own = pair[0].reshape(rows, npro)
        q_oth = pair[1].reshape(rows, npro)

        def tdot(a, b):
            return lax.dot_general(a, b, (((0,), (0,)), ((), ())), preferred_element_type=f32)

        mirrored = tdot(own, q_own) + tdot(oth, q_oth)
        m0 = mirrored[:fine]
        ms = mirrored[fine:].astype(bf16)
        total = m0
        for d in range(nz - 1, 0, -1):
            total = total + lax.ppermute(ms[(d - 1) * fine : d * fine], both, up(d)).astype(f32)

        d_own = jnp.dot(own, pcat, preferred_element_type=f32).reshape(nx, nk, fine, npro)
        d_oth = jnp.dot(oth, pcat, preferred_element_type=f32).reshape(nx, nk, fine, npro)
        d_all = jnp.stack([d_own, d_oth])
        keep = lax.dynamic_index_in_dim(d_all, k, 2, keepdims=False)
        part = keep + lax.ppermute(
            lax.dynamic_index_in_dim(d_all, 1 - k, 2, keepdims=False).astype(bf16), both, other_core
        ).astype(f32)
        total = total + lax.dynamic_index_in_dim(part[0], x, 0, keepdims=False)
        for s, e in away:
            piece = lax.dynamic_index_in_dim(part[s], (x + e) % nx, 0, keepdims=False).astype(bf16)
            total = total + lax.ppermute(piece, both, shift(s, e)).astype(f32)
        pf = probes.astype(f32)
        total = total + diag[:, None] * pf
        return components[0] * total + components[1] * pf

    return jax.shard_map(
        body,
        mesh=mesh,
        in_specs=(P("row", None, "col", None), P(both, None), P(both), P()),
        out_specs=P(both, None),
        check_vma=False,
    )
```

```python
import functools

import jax
import jax.numpy as jnp
from jax import lax
from jax.experimental import pallas as pl
from jax.experimental.pallas import tpu as pltpu
from jax.sharding import PartitionSpec as P

F32, BF16, I32 = jnp.float32, jnp.bfloat16, jnp.int32
VMEM_LIMIT = 56 * 1024 * 1024


def iota(shape, dim):
    return lax.broadcasted_iota(I32, shape, dim)


def call(kernel, outs, *args, vmem=None):
    specs = [pl.BlockSpec(memory_space=pltpu.SMEM)] + [pl.BlockSpec(memory_space=pltpu.VMEM)] * (len(args) - 1)
    return pl.pallas_call(
        kernel,
        out_shape=[jax.ShapeDtypeStruct(s, d) for s, d in outs],
        in_specs=specs,
        out_specs=[pl.BlockSpec(memory_space=pltpu.VMEM)] * len(outs),
        scratch_shapes=vmem or [],
        compiler_params=pltpu.CompilerParams(vmem_limit_bytes=VMEM_LIMIT),
    )(*args)


def tdot(a, b):
    return lax.dot_general(a, b, (((0,), (0,)), ((), ())), preferred_element_type=F32)


def dot(a, b):
    return jnp.dot(a, b, preferred_element_type=F32)


def prep_kernel(at, u, signs, weights, probes, own, give, diag, *, nz, ny, fine, rows):
    z, y, c = at[0], at[1], at[2]
    ntiles = nz * ny
    take = 256 // ntiles
    eye = iota((fine, fine), 0) == iota((fine, fine), 1)
    wcol = jnp.sum(jnp.where(eye, weights[...], 0.0), axis=1, keepdims=True)
    probes[...] = ((2 * signs[...] - 1).astype(F32) * wcol).astype(BF16)
    j, m = iota((256, 256), 0), iota((256, 256), 1)
    slot, i = j // take, j % take
    d = slot % nz
    side = jnp.where(slot < nz, y, 1 - y)
    tile = ((z + d) % nz) * ny + side
    pick = jnp.where(m == i * ntiles + tile, 1.0, 0.0).astype(BF16)
    for h in range(rows // (2 * take)):
        x = jnp.concatenate([u[h * 512 : h * 512 + 256, :], u[h * 512 + 256 : h * 512 + 512, :]], axis=1)
        o = dot(pick, x).astype(BF16)
        for g in range(2):
            r0 = h * 2 * take + g * take
            og = o[:, g * fine : (g + 1) * fine]
            for s in range(nz):
                part = og[s * take : (s + 1) * take]
                mirror = og[(nz + s) * take : (nz + s + 1) * take]
                if s == 0:
                    col = c * fine + iota((take, fine), 1)
                    row = r0 + iota((take, fine), 0)
                    own[r0 : r0 + take, 0:fine] = jnp.where(col > row, part.astype(F32), 0.0).astype(BF16)
                    own[r0 : r0 + take, nz * fine : (nz + 1) * fine] = jnp.where(
                        y == 0, mirror.astype(F32), 0.0
                    ).astype(BF16)
                else:
                    own[r0 : r0 + take, s * fine : (s + 1) * fine] = part
                    give[r0 : r0 + take, (s - 1) * fine : s * fine] = mirror
    base = c * fine * ntiles
    t = z * ny + y
    blk = u[pl.ds(pl.multiple_of(base, 128), fine * ntiles), :].astype(F32)
    a, b = iota((fine * ntiles, fine), 0), iota((fine * ntiles, fine), 1)
    picked = jnp.where(a == b * ntiles + t, blk, 0.0)
    row = jnp.sum(picked, axis=0, keepdims=True)
    diag[...] = jnp.broadcast_to(jnp.sum(jnp.where(eye, row, 0.0), axis=1, keepdims=True), (fine, fine))


def mirror_kernel(at, own, oth, near, far, m0, mx, ms, q, *, nz, ny, nx, nk, fine):
    x, k = at[3], at[4]
    rows = nx * nk * fine
    for s in range(ny):
        for e in range(nx):
            xx = (x + e) % nx
            i = s * nx + e
            q[s, pl.ds(pl.multiple_of((xx * nk + k) * fine, fine), fine), :] = near[i]
            q[s, pl.ds(pl.multiple_of((xx * nk + 1 - k) * fine, fine), fine), :] = far[i]
    q0, q1 = q[0], q[1]
    m0[...] = tdot(own[:, :fine], q0)
    mx[...] = tdot(own[:, nz * fine :], q0)
    ms[...] = (tdot(own[:, fine : nz * fine], q0) + tdot(oth[...], q1)).astype(BF16).reshape(ms.shape)


def direct_kernel(at, own, oth, mx, *refs, nz, ny, nx, nk, fine):
    ps, (keep, send), (p, d) = refs[: nz + 1], refs[nz + 1 : nz + 3], refs[nz + 3 :]
    k = at[4]
    x = at[3]
    npro = p.shape[1]
    for n in range(nz + 1):
        p[n * fine : (n + 1) * fine, :] = ps[n][...]
    d[0] = dot(own[...], p[...])
    d[1] = dot(oth[...], p[fine : nz * fine, :])
    mine = pl.ds(pl.multiple_of((x * nk + k) * fine, fine), fine)
    d[1, mine, :] = d[1, mine, :] + mx[...]
    for s in range(ny):
        for e in range(nx):
            xx = (x + e) % nx
            i = s * nx + e
            keep[i] = d[s, pl.ds(pl.multiple_of((xx * nk + k) * fine, fine), fine), :]
            send[i] = d[s, pl.ds(pl.multiple_of((xx * nk + 1 - k) * fine, fine), fine), :].astype(BF16)


def fold_kernel(at, keep, got, home, *pieces, nx, ny):
    home[...] = keep[0] + got[0].astype(F32)
    for i in range(1, nx * ny):
        pieces[i - 1][...] = (keep[i] + got[i].astype(F32)).astype(BF16)


def last_kernel(comp, probes, diag, m0, home, *refs):
    out = refs[-1]
    total = m0[...] + home[...]
    for r in refs[:-1]:
        total = total + r[...].astype(F32)
    pf = probes[...].astype(F32)
    total = total + diag[:, 0:1] * pf
    out[...] = comp[0] * total + comp[1] * pf


def solution(mesh):
    nrow, ncol = mesh.shape["row"], mesh.shape["col"]
    ny, nk = 2, 2
    nz, nx = nrow // ny, ncol // nk
    both = ("row", "col")

    def place(z, y, x, k):
        return ((z * ny + y) * nx + x) * nk + k

    spots = [(z, y, x, k) for z in range(nz) for y in range(ny) for x in range(nx) for k in range(nk)]

    def down(d):
        return [(place(z, y, x, k), place(z - d, y, x, k)) for z, y, x, k in spots if z >= d]

    def up(d):
        return [(place(z, y, x, k), place(z + d, y, x, k)) for z, y, x, k in spots if z + d < nz]

    def shift(s, e):
        return [(place(z, y, x, k), place(z, y ^ s, (x + e) % nx, k)) for z, y, x, k in spots]

    other_core = [(place(z, y, x, k), place(z, y, x, 1 - k)) for z, y, x, k in spots]
    away = [(s, e) for s in range(ny) for e in range(nx) if (s, e) != (0, 0)]

    def body(upper, signs, weights, components):
        rows, ntiles, _, fine = upper.shape
        npro = signs.shape[1]
        r, c = lax.axis_index("row"), lax.axis_index("col")
        z, y, x, k = r // ny, r % ny, c // nk, c % nk
        at = jnp.stack([z, y, c, x, k]).astype(I32)
        blk = (fine, npro)
        nblk = nx * ny

        probes, own, give, diag = call(
            functools.partial(prep_kernel, nz=nz, ny=ny, fine=fine, rows=rows),
            [(blk, BF16), ((rows, (nz + 1) * fine), BF16), ((rows, (nz - 1) * fine), BF16), ((fine, fine), F32)],
            at, upper.reshape(rows * ntiles, fine), signs, weights.reshape(1, fine),
        )
        downs = {d: lax.ppermute(probes, both, down(d)) for d in range(nz - 1, 0, -1)}
        oth = lax.ppermute(give, both, shift(1, 0))
        near = [probes] + [lax.ppermute(probes, both, shift(s, (nx - e) % nx)) for s, e in away]
        near = jnp.stack(near)
        far = lax.ppermute(near, both, other_core)
        m0, mx, ms = call(
            functools.partial(mirror_kernel, nz=nz, ny=ny, nx=nx, nk=nk, fine=fine),
            [(blk, F32), (blk, F32), ((nz - 1, *blk), BF16)],
            at, own, oth, near, far,
            vmem=[pltpu.VMEM((ny, rows, npro), BF16)],
        )
        ups = [lax.ppermute(ms[d - 1], both, up(d)) for d in range(nz - 1, 0, -1)]
        keep, send = call(
            functools.partial(direct_kernel, nz=nz, ny=ny, nx=nx, nk=nk, fine=fine),
            [((nblk, *blk), F32), ((nblk, *blk), BF16)],
            at, own, oth, mx, probes, *[downs[d] for d in range(1, nz)], near[nx],
            vmem=[pltpu.VMEM(((nz + 1) * fine, npro), BF16), pltpu.VMEM((ny, rows, npro), F32)],
        )
        got = lax.ppermute(send, both, other_core)
        home, *pieces = call(
            functools.partial(fold_kernel, nx=nx, ny=ny),
            [(blk, F32)] + [(blk, BF16)] * (nblk - 1),
            at, keep, got,
        )
        cross = [lax.ppermute(p, both, shift(s, e)) for p, (s, e) in zip(pieces, away)]
        (out,) = call(last_kernel, [(blk, F32)], components, probes, diag, m0, home, *cross, *ups)
        return out

    return jax.shard_map(
        body,
        mesh=mesh,
        in_specs=(P("row", None, "col", None), P(both, None), P(both), P()),
        out_specs=P(both, None),
        check_vma=False,
    )
```

```python
import functools
import math

import jax
import jax.numpy as jnp
from jax import lax
from jax.experimental import pallas as pl
from jax.experimental.pallas import tpu as pltpu
from jax.sharding import PartitionSpec as P

F32, BF16, I32 = jnp.float32, jnp.bfloat16, jnp.int32
ROOM = 12 * 1024 * 1024


def iota(shape, dim):
    return lax.broadcasted_iota(I32, shape, dim)


def call(kernel, outs, *args, hbm=(), scratch=()):
    spaces = [pltpu.HBM if i in hbm else pltpu.VMEM for i in range(len(args))]
    specs = [pl.BlockSpec(memory_space=m) for m in spaces]
    ops = [pltpu.with_memory_space_constraint(a, m) for a, m in zip(args, spaces)]
    held = sum(math.prod(m.shape) * jnp.dtype(m.dtype).itemsize for m in scratch if m.memory_space == pltpu.VMEM)
    return pl.pallas_call(
        kernel,
        out_shape=outs,
        in_specs=specs,
        out_specs=[pl.BlockSpec(memory_space=pltpu.VMEM)] * len(outs),
        scratch_shapes=list(scratch),
        cost_estimate=pl.CostEstimate(flops=1, bytes_accessed=1, transcendentals=0),
        compiler_params=pltpu.CompilerParams(vmem_limit_bytes=held + ROOM),
    )(*ops)


def tdot(a, b):
    return lax.dot_general(a, b, (((0,), (0,)), ((), ())), preferred_element_type=F32)


def dot(a, b):
    return jnp.dot(a, b, preferred_element_type=F32)


def where_am_i(ny, nk):
    r, c = lax.axis_index("row"), lax.axis_index("col")
    return r // ny, r % ny, c, c // nk, c % nk


def prep_kernel(u_hbm, comp_hbm, own, give, diag, scale, u, comp, raw, sems, *, nz, ny, nk, fine, rows):
    z, y, c, _, _ = where_am_i(ny, nk)
    ntiles = nz * ny
    take = 256 // ntiles
    parts = rows // (2 * take)
    get_comp = pltpu.make_async_copy(comp_hbm, comp, sems.at[0])
    get_u = pltpu.make_async_copy(u_hbm, u, sems.at[1])
    get_u.start()
    get_comp.start()
    j, m = iota((256, 256), 0), iota((256, 256), 1)
    slot, i = j // take, j % take
    d = slot % nz
    side = jnp.where(slot < nz, y, 1 - y)
    tile = ((z + d) % nz) * ny + side
    pick = jnp.where(m == i * ntiles + tile, 1.0, 0.0).astype(BF16)
    eye = iota((fine, fine), 0) == iota((fine, fine), 1)
    get_comp.wait()
    scale[0:1, :] = jnp.broadcast_to(comp[0:1, 0:1], (1, fine))
    scale[1:2, :] = jnp.broadcast_to(comp[0:1, 1:2], (1, fine))
    get_u.wait()
    for h in range(parts):
        x = jnp.concatenate([u[h * 512 : h * 512 + 256, :], u[h * 512 + 256 : h * 512 + 512, :]], axis=1)
        o = dot(pick, x)
        for g in range(2):
            r0 = h * 2 * take + g * take
            og = o[:, g * fine : (g + 1) * fine]
            for s in range(nz):
                part = og[s * take : (s + 1) * take]
                mirror = og[(nz + s) * take : (nz + s + 1) * take]
                if s == 0:
                    col = c * fine + iota((take, fine), 1)
                    row = r0 + iota((take, fine), 0)
                    raw[r0 : r0 + take, :] = part
                    own[r0 : r0 + take, 0:fine] = jnp.where(col > row, part, 0.0).astype(BF16)
                    own[r0 : r0 + take, nz * fine : (nz + 1) * fine] = jnp.where(y == 0, mirror, 0.0).astype(BF16)
                else:
                    own[r0 : r0 + take, s * fine : (s + 1) * fine] = part.astype(BF16)
                    give[r0 : r0 + take, (s - 1) * fine : s * fine] = mirror.astype(BF16)
    blk = raw[pl.ds(pl.multiple_of(c * fine, fine), fine), :]
    diag[...] = jnp.broadcast_to(jnp.sum(jnp.where(eye, blk, 0.0), axis=1, keepdims=True), (fine, fine))


def relay_kernel(probes, got, out, *, ny, nk):
    z = where_am_i(ny, nk)[0]

    @pl.when(z == 1)
    def _():
        out[...] = got[...]

    @pl.when(z != 1)
    def _():
        out[...] = probes[...]


def stack_kernel(*refs):
    for i, r in enumerate(refs[:-1]):
        refs[-1][i] = r[...]


def direct_kernel(own, oth, *refs, nz, ny, nx, nk, fine):
    ps, (keep, send, p, d) = refs[: nz + 1], refs[nz + 1 :]
    z, _, _, x, k = where_am_i(ny, nk)
    for n in range(nz + 1):
        p[n * fine : (n + 1) * fine, :] = ps[n][...]
    if nz == 4:
        @pl.when(z == 1)
        def _():
            p[fine : 2 * fine, :] = ps[3][...]
            p[3 * fine : 4 * fine, :] = jnp.zeros_like(ps[3][...])

    d[0] = dot(own[...], p[...])
    d[1] = dot(oth[...], p[fine : nz * fine, :])
    for s in range(ny):
        for e in range(nx):
            xx = (x + e) % nx
            i = s * nx + e
            keep[i] = d[s, pl.ds(pl.multiple_of((xx * nk + k) * fine, fine), fine), :]
            send[i] = d[s, pl.ds(pl.multiple_of((xx * nk + 1 - k) * fine, fine), fine), :].astype(BF16)


def mirror_kernel(own, oth, near, far, keep, m0, mx, *refs, nz, ny, nx, nk, fine):
    ms, q = refs[:-1], refs[-1]
    _, _, _, x, k = where_am_i(ny, nk)
    for s in range(ny):
        for e in range(nx):
            xx = (x + e) % nx
            i = s * nx + e
            q[s, pl.ds(pl.multiple_of((xx * nk + k) * fine, fine), fine), :] = near[i]
            q[s, pl.ds(pl.multiple_of((xx * nk + 1 - k) * fine, fine), fine), :] = far[i]
    q0, q1 = q[0], q[1]
    mo = tdot(own[...], q0)
    m0[...] = mo[:fine]
    mx[...] = mo[nz * fine :]
    md = (mo[fine : nz * fine] + tdot(oth[...], q1)).astype(BF16)
    for d in range(nz - 1):
        ms[d][...] = md[d * fine : (d + 1) * fine]


def fold_kernel(keep, got, mx, *refs, nx, ny, nz):
    near_ms, home, pieces, out_ms = refs[: nz - 2], refs[nz - 2], refs[nz - 1 : nz + nx * ny - 2], refs[nz + nx * ny - 2 :]
    home[...] = keep[0] + got[0].astype(F32)
    for i in range(1, nx * ny):
        total = keep[i] + got[i].astype(F32)
        if i == nx:
            total = total + mx[...]
        pieces[i - 1][...] = total.astype(BF16)
    for a, b in zip(near_ms, out_ms):
        b[...] = a[...]


def last_kernel(comp, probes, diag, m0, home, *refs):
    out = refs[-1]
    total = m0[...] + home[...]
    for r in refs[:-1]:
        total = total + r[...].astype(F32)
    pf = probes[...].astype(F32)
    total = total + diag[:, 0:1] * pf
    out[...] = comp[0:1, 0:1] * total + comp[1:2, 0:1] * pf


def solution(mesh):
    nrow, ncol = mesh.shape["row"], mesh.shape["col"]
    ny, nk = 2, 2
    nz, nx = nrow // ny, ncol // nk
    both = ("row", "col")

    def place(z, y, x, k):
        return ((z * ny + y) * nx + x) * nk + k

    spots = [(z, y, x, k) for z in range(nz) for y in range(ny) for x in range(nx) for k in range(nk)]

    def down(d):
        return [(place(z, y, x, k), place(z - d, y, x, k)) for z, y, x, k in spots if z >= d]

    def up(d):
        return [(place(z, y, x, k), place(z + d, y, x, k)) for z, y, x, k in spots if z + d < nz]

    def hop(*steps):
        return [(place(a, y, x, k), place(b, y, x, k)) for a, b in steps for z, y, x, k in spots if z == 0]

    def shift(s, e):
        return [(place(z, y, x, k), place(z, y ^ s, (x + e) % nx, k)) for z, y, x, k in spots]

    other_core = [(place(z, y, x, k), place(z, y, x, 1 - k)) for z, y, x, k in spots]
    away = [(s, e) for s in range(ny) for e in range(nx) if (s, e) != (0, 0)]

    def body(upper, signs, weights, components):
        rows, ntiles, _, fine = upper.shape
        npro = signs.shape[1]
        blk = (fine, npro)
        nblk = nx * ny

        probes = ((2 * signs - 1).astype(F32) * weights[:, None]).astype(BF16)
        if nz == 4:
            first = lax.ppermute(probes, both, hop((3, 0), (2, 1)))
        near = {(0, 0): probes}
        for s, e in reversed(away):
            near[s, e] = lax.ppermute(probes, both, shift(s, (nx - e) % nx))
        own, give, diag, scale = call(
            functools.partial(prep_kernel, nz=nz, ny=ny, nk=nk, fine=fine, rows=rows),
            [
                pltpu.VMEM((rows, (nz + 1) * fine), BF16),
                pltpu.VMEM((rows, (nz - 1) * fine), BF16),
                pltpu.VMEM((fine, fine), F32),
                pltpu.VMEM((2, fine), F32),
            ],
            upper.reshape(rows * ntiles, fine), components.reshape(1, 2),
            hbm=(0, 1),
            scratch=[
                pltpu.VMEM((rows * ntiles, fine), BF16),
                pltpu.VMEM((1, 2), F32),
                pltpu.VMEM((rows, fine), F32),
                pltpu.SemaphoreType.DMA((2,)),
            ],
        )
        oth = lax.ppermute(give, both, shift(1, 0))
        if nz == 4:
            downs = {1: lax.ppermute(probes, both, hop((3, 2), (1, 0))), 3: first}
            (later,) = call(functools.partial(relay_kernel, ny=ny, nk=nk), [pltpu.VMEM(blk, BF16)], probes, first)
            downs[2] = lax.ppermute(later, both, hop((3, 1), (1, 0)))
        else:
            downs = {d: lax.ppermute(probes, both, down(d)) for d in range(nz - 1, 0, -1)}
        (stack,) = call(
            stack_kernel, [pltpu.VMEM((nblk, *blk), BF16)], *[near[s, e] for s in range(ny) for e in range(nx)]
        )
        far = lax.ppermute(stack, both, other_core)
        oth, downs = lax.optimization_barrier((oth, downs))
        keep, send = call(
            functools.partial(direct_kernel, nz=nz, ny=ny, nx=nx, nk=nk, fine=fine),
            [pltpu.VMEM((nblk, *blk), F32), pltpu.VMEM((nblk, *blk), BF16)],
            own, oth, probes, *[downs[d] for d in range(1, nz)], near[1, 0],
            scratch=[pltpu.VMEM(((nz + 1) * fine, npro), BF16), pltpu.VMEM((ny, rows, npro), F32)],
        )
        got = lax.ppermute(send, both, other_core)
        m0, mx, *ms = call(
            functools.partial(mirror_kernel, nz=nz, ny=ny, nx=nx, nk=nk, fine=fine),
            [pltpu.VMEM(blk, F32), pltpu.VMEM(blk, F32)] + [pltpu.VMEM(blk, BF16)] * (nz - 1),
            own, oth, stack, far, keep,
            scratch=[pltpu.VMEM((ny, rows, npro), BF16)],
        )
        ups = [lax.ppermute(ms[nz - 2], both, up(nz - 1))]
        home, *rest = call(
            functools.partial(fold_kernel, nx=nx, ny=ny, nz=nz),
            [pltpu.VMEM(blk, F32)] + [pltpu.VMEM(blk, BF16)] * (nblk - 1 + nz - 2),
            keep, got, mx, *ms[: nz - 2],
        )
        pieces, ms = rest[: nblk - 1], rest[nblk - 1 :]
        cross = [lax.ppermute(p, both, shift(s, e)) for p, (s, e) in zip(pieces, away)]
        ups += [lax.ppermute(ms[d - 1], both, up(d)) for d in range(nz - 2, 0, -1)]
        (out,) = call(
            last_kernel, [jax.ShapeDtypeStruct(blk, F32)],
            scale, probes, diag, m0, home, *cross, *ups,
        )
        return out

    return jax.shard_map(
        body,
        mesh=mesh,
        in_specs=(P("row", None, "col", None), P(both, None), P(both), P()),
        out_specs=P(both, None),
        check_vma=False,
    )
```

```python
import functools
import math

import jax
import jax.numpy as jnp
from jax import lax
from jax.experimental import pallas as pl
from jax.experimental.pallas import tpu as pltpu
from jax.sharding import PartitionSpec as P

F32, BF16, I32 = jnp.float32, jnp.bfloat16, jnp.int32
ROOM = 12 * 1024 * 1024


def iota(shape, dim):
    return lax.broadcasted_iota(I32, shape, dim)


def call(kernel, outs, *args, hbm=(), scratch=(), order=None):
    if order is not None:
        inner, place = kernel, [order.index(i) for i in range(len(args))]

        def kernel(*refs):
            inner(*[refs[i] for i in place], *refs[len(place) :])

        args = [args[i] for i in order]
    spaces = [pltpu.HBM if i in hbm else pltpu.VMEM for i in range(len(args))]
    specs = [pl.BlockSpec(memory_space=m) for m in spaces]
    ops = [pltpu.with_memory_space_constraint(a, m) for a, m in zip(args, spaces)]
    held = sum(math.prod(m.shape) * jnp.dtype(m.dtype).itemsize for m in scratch if m.memory_space == pltpu.VMEM)
    return pl.pallas_call(
        kernel,
        out_shape=outs,
        in_specs=specs,
        out_specs=[pl.BlockSpec(memory_space=pltpu.VMEM)] * len(outs),
        scratch_shapes=list(scratch),
        cost_estimate=pl.CostEstimate(flops=1, bytes_accessed=1, transcendentals=0),
        compiler_params=pltpu.CompilerParams(vmem_limit_bytes=held + ROOM),
    )(*ops)


def tdot(a, b):
    return lax.dot_general(a, b, (((0,), (0,)), ((), ())), preferred_element_type=F32)


def dot(a, b):
    return jnp.dot(a, b, preferred_element_type=F32)


def where_am_i(ny, nk):
    r, c = lax.axis_index("row"), lax.axis_index("col")
    return r // ny, r % ny, c, c // nk, c % nk


def packed(row, fine, wide):
    block = row // fine
    return (1 + block // wide) * fine + row % fine, block % wide * fine


def prep_kernel(
    u_hbm, signs_hbm, weights_hbm, comp_hbm,
    probes, own, give1, give2, diag, scale,
    u, signs, weights, comp, raw, sems,
    *, nz, ny, nk, fine, rows,
):
    z, y, c, _, _ = where_am_i(ny, nk)
    ntiles = nz * ny
    take = 256 // ntiles
    parts = rows // (2 * take)
    wide = probes.shape[1] // fine
    pairs = [(signs_hbm, signs), (weights_hbm, weights), (u_hbm, u), (comp_hbm, comp)]
    gets = [pltpu.make_async_copy(a, b, sems.at[n]) for n, (a, b) in enumerate(pairs)]
    for g in gets:
        g.start()
    j, m = iota((256, 256), 0), iota((256, 256), 1)
    slot, i = j // take, j % take
    d = slot % nz
    side = jnp.where(slot < nz, y, 1 - y)
    tile = ((z + d) % nz) * ny + side
    pick = jnp.where(m == i * ntiles + tile, 1.0, 0.0).astype(BF16)
    eye = iota((fine, fine), 0) == iota((fine, fine), 1)
    gets[0].wait()
    gets[1].wait()
    wcol = jnp.sum(jnp.where(eye, weights[...], 0.0), axis=1, keepdims=True)
    pv = ((2 * signs[...] - 1).astype(F32) * wcol).astype(BF16)
    probes[...] = pv
    give1[0:fine, :] = pv
    gets[3].wait()
    scale[0:1, :] = jnp.broadcast_to(comp[0:1, 0:1], (1, fine))
    scale[1:2, :] = jnp.broadcast_to(comp[0:1, 1:2], (1, fine))
    gets[2].wait()
    for h in range(parts):
        x = jnp.concatenate([u[h * 512 : h * 512 + 256, :], u[h * 512 + 256 : h * 512 + 512, :]], axis=1)
        o = dot(pick, x)
        for g in range(2):
            r0 = h * 2 * take + g * take
            og = o[:, g * fine : (g + 1) * fine]
            for s in range(nz):
                part = og[s * take : (s + 1) * take]
                mirror = og[(nz + s) * take : (nz + s + 1) * take]
                if s == 0:
                    col = c * fine + iota((take, fine), 1)
                    row = r0 + iota((take, fine), 0)
                    raw[r0 : r0 + take, :] = part
                    own[r0 : r0 + take, 0:fine] = jnp.where(col > row, part, 0.0).astype(BF16)
                    own[r0 : r0 + take, nz * fine : (nz + 1) * fine] = jnp.where(y == 0, mirror, 0.0).astype(BF16)
                else:
                    own[r0 : r0 + take, s * fine : (s + 1) * fine] = part.astype(BF16)
                    if s > 1:
                        give2[r0 : r0 + take, (s - 2) * fine : (s - 1) * fine] = mirror.astype(BF16)
                    else:
                        top, left = packed(r0, fine, wide)
                        give1[top : top + take, left : left + fine] = mirror.astype(BF16)
    blk = raw[pl.ds(pl.multiple_of(c * fine, fine), fine), :]
    diag[...] = jnp.broadcast_to(jnp.sum(jnp.where(eye, blk, 0.0), axis=1, keepdims=True), (fine, fine))


def relay_kernel(*refs):
    out = refs[-1]
    out[...] = refs[0][0 : out.shape[0], :]


def stack_kernel(*refs, order):
    for i, r in zip(order, refs[:-1]):
        refs[-1][i] = r[0 : refs[-1].shape[1], :]


def direct_kernel(own, oth1, oth2, *refs, nz, ny, nx, nk, fine):
    ps, (keep, send, oth, p, d) = refs[: nz + 1], refs[nz + 1 :]
    _, _, _, x, k = where_am_i(ny, nk)
    for n in range(nz + 1):
        p[n * fine : (n + 1) * fine, :] = ps[n][0:fine, :]
    d[0] = dot(own[...], p[...])
    for r0 in range(0, oth.shape[0], fine):
        top, left = packed(r0, fine, p.shape[1] // fine)
        oth[r0 : r0 + fine, 0:fine] = oth1[top : top + fine, left : left + fine]
    oth[:, fine:] = oth2[...]
    d[1] = dot(oth[...], p[fine : nz * fine, :])
    for s in range(ny):
        for e in range(nx):
            xx = (x + e) % nx
            i = s * nx + e
            keep[i] = d[s, pl.ds(pl.multiple_of((xx * nk + k) * fine, fine), fine), :]
            send[i] = d[s, pl.ds(pl.multiple_of((xx * nk + 1 - k) * fine, fine), fine), :].astype(BF16)


def mirror_kernel(near, far, keep, own, oth, m0, mx, *refs, nz, ny, nx, nk, fine):
    ms, q = refs[:-1], refs[-1]
    _, _, _, x, k = where_am_i(ny, nk)
    for s in range(ny):
        for e in range(nx):
            xx = (x + e) % nx
            i = s * nx + e
            q[s, pl.ds(pl.multiple_of((xx * nk + k) * fine, fine), fine), :] = near[i]
            q[s, pl.ds(pl.multiple_of((xx * nk + 1 - k) * fine, fine), fine), :] = far[i]
    q0, q1 = q[0], q[1]
    mo = tdot(own[...], q0)
    m0[...] = mo[:fine]
    mx[...] = mo[nz * fine :]
    md = (mo[fine : nz * fine] + tdot(oth[...], q1)).astype(BF16)
    for d in range(1, nz):
        ms[d - 1][...] = md[(d - 1) * fine : d * fine]


def fold_kernel(keep, got, mx, *refs, nx, ny):
    n = (len(refs) - nx * ny) // 2
    held, home, pieces, passed = refs[:n], refs[n], refs[n + 1 : n + nx * ny], refs[n + nx * ny :]
    home[...] = keep[0] + got[0].astype(F32)
    for i in range(1, nx * ny):
        total = keep[i] + got[i].astype(F32)
        if i == nx:
            total = total + mx[...]
        pieces[i - 1][...] = total.astype(BF16)
    for a, b in zip(held, passed):
        b[...] = a[...]


def last_kernel(scale, probes, diag, *refs):
    out = refs[-1]
    total = refs[0][...].astype(F32)
    for r in refs[1:-1]:
        total = total + r[...].astype(F32)
    pf = probes[...].astype(F32)
    total = total + diag[:, 0:1] * pf
    out[...] = scale[0:1, 0:1] * total + scale[1:2, 0:1] * pf


def solution(mesh):
    nrow, ncol = mesh.shape["row"], mesh.shape["col"]
    ny, nk = 2, 2
    nz, nx = nrow // ny, ncol // nk
    both = ("row", "col")

    def place(z, y, x, k):
        return ((z * ny + y) * nx + x) * nk + k

    spots = [(z, y, x, k) for z in range(nz) for y in range(ny) for x in range(nx) for k in range(nk)]

    def down(d):
        return [(place(z, y, x, k), place(z - d, y, x, k)) for z, y, x, k in spots if z >= d]

    def up(d):
        return [(place(z, y, x, k), place(z + d, y, x, k)) for z, y, x, k in spots if z + d < nz]

    def hop(*steps):
        return [(place(a, y, x, k), place(b, y, x, k)) for a, b in steps for z, y, x, k in spots if z == 0]

    def shift(s, e):
        return [(place(z, y, x, k), place(z, y ^ s, (x + e) % nx, k)) for z, y, x, k in spots]

    other_core = [(place(z, y, x, k), place(z, y, x, 1 - k)) for z, y, x, k in spots]
    away = [(s, e) for s in range(ny) for e in range(nx) if (s, e) != (0, 0)]

    def body(upper, signs, weights, components):
        rows, ntiles, _, fine = upper.shape
        npro = signs.shape[1]
        blk = (fine, npro)
        nblk = nx * ny

        probes, own, give1, give2, diag, scale = call(
            functools.partial(prep_kernel, nz=nz, ny=ny, nk=nk, fine=fine, rows=rows),
            [
                pltpu.VMEM(blk, BF16),
                pltpu.VMEM((rows, (nz + 1) * fine), BF16),
                pltpu.VMEM((fine + rows * fine // npro, npro), BF16),
                pltpu.VMEM((rows, (nz - 2) * fine), BF16),
                pltpu.VMEM((fine, fine), F32),
                pltpu.VMEM((2, fine), F32),
            ],
            upper.reshape(rows * ntiles, fine), signs, weights.reshape(1, fine), components.reshape(1, 2),
            hbm=(0, 1, 2, 3),
            scratch=[
                pltpu.VMEM((rows * ntiles, fine), BF16),
                pltpu.VMEM(blk, I32),
                pltpu.VMEM((1, fine), F32),
                pltpu.VMEM((1, 2), F32),
                pltpu.VMEM((rows, fine), F32),
                pltpu.SemaphoreType.DMA((4,)),
            ],
        )
        oth1 = lax.ppermute(give1, both, shift(1, 0))
        downs = {1: lax.ppermute(probes, both, down(1))}
        pairs = [(a, b) for a, b in shift(1, 0) if a // (ny * nx * nk) < nz - 2]
        oth2 = lax.ppermute(give2, both, pairs)
        if nz == 4:
            downs[3] = lax.ppermute(probes, both, down(3))
        near = {(0, 0): probes}
        for e in range(1, nx):
            near[0, e] = lax.ppermute(probes, both, shift(0, nx - e))
        have = {"a": downs[1], "x": near[0, 1], "y": oth1, "b": downs.get(3, downs[1])}
        (pad,) = call(
            relay_kernel, [pltpu.VMEM(blk, BF16)], oth1, *[have[n] for n in 'ax']
        )
        near[1, 0] = pad
        for e in range(1, nx):
            near[1, e] = lax.ppermute(pad, both, shift(0, nx - e))
        if nz == 4:
            handed = downs[1]
            if 'xyb':
                (handed,) = call(relay_kernel, [pltpu.VMEM(blk, BF16)], handed, *[have[n] for n in 'xyb'])
            downs[2] = lax.ppermute(handed, both, hop((2, 1), (1, 0)))
        else:
            downs |= {d: lax.ppermute(probes, both, down(d)) for d in range(2, nz)}
        order = [(s, e) for s in range(ny) for e in range(nx)]
        if nz == 4:
            order = [order[i] for i in [2, 0, 1, 3]]
        (stack,) = call(
            functools.partial(stack_kernel, order=[s * nx + e for s, e in order]),
            [pltpu.VMEM((nblk, *blk), BF16)],
            *[near[p] for p in order],
        )
        far = lax.ppermute(stack, both, other_core)
        oth2, downs = lax.optimization_barrier((oth2, downs))
        keep, send, oth = call(
            functools.partial(direct_kernel, nz=nz, ny=ny, nx=nx, nk=nk, fine=fine),
            [pltpu.VMEM((nblk, *blk), F32), pltpu.VMEM((nblk, *blk), BF16), pltpu.VMEM((rows, (nz - 1) * fine), BF16)],
            own, oth1, oth2, probes, *[downs[d] for d in range(1, nz)], near[1, 0],
            scratch=[pltpu.VMEM(((nz + 1) * fine, npro), BF16), pltpu.VMEM((ny, rows, npro), F32)],
            order=[0, 1, 2, 3, 4, 5, 6, 7] if nz == 4 else None,
        )
        got = lax.ppermute(send, both, other_core)
        m0, mx, *ms = call(
            functools.partial(mirror_kernel, nz=nz, ny=ny, nx=nx, nk=nk, fine=fine),
            [pltpu.VMEM(blk, F32), pltpu.VMEM(blk, F32)] + [pltpu.VMEM(blk, BF16)] * (nz - 1),
            stack, far, keep, own, oth,
            scratch=[pltpu.VMEM((ny, rows, npro), BF16)],
            order=[0, 1, 2, 3, 4] if nz == 4 else None,
        )
        steps = [1, 2, 3] if nz == 4 else list(range(1, nz))
        direct, chain = (1, 1) if nz == 4 else (1, False)
        climbs = [[(z, z + d) for z in range(nz - d)] for d in steps]
        ups = [lax.ppermute(ms[d - 1], both, hop(*climbs[i])) for i, d in enumerate(steps) if i < direct]
        home, *rest = call(
            functools.partial(fold_kernel, nx=nx, ny=ny),
            [pltpu.VMEM(blk, F32)] + [pltpu.VMEM(blk, BF16)] * (nblk - 1 + nz - 1 - direct),
            keep, got, mx, *[ms[d - 1] for d in steps[direct:]],
        )
        pieces, held = rest[: nblk - 1], rest[nblk - 1 :]
        cross = [lax.ppermute(p, both, shift(s, e)) for p, (s, e) in zip(pieces, away)]
        for n, h in enumerate(held):
            if chain and n == len(held) - 1:
                (h,) = call(relay_kernel, [pltpu.VMEM(blk, BF16)], h, ups[0])
            ups.append(lax.ppermute(h, both, hop(*climbs[direct + n])))
        tail = [scale, probes, diag, m0, home, *ups, *cross]
        (out,) = call(
            last_kernel, [jax.ShapeDtypeStruct(blk, F32)], *tail,
            order=[4, 1, 0, 5, 7, 2, 10, 6, 3, 8, 9] if nz == 4 else None,
        )
        return out

    return jax.shard_map(
        body,
        mesh=mesh,
        in_specs=(P("row", None, "col", None), P(both, None), P(both), P()),
        out_specs=P(both, None),
        check_vma=False,
    )
```

```python
import functools
import math

import jax
import jax.numpy as jnp
from jax import lax
from jax.experimental import pallas as pl
from jax.experimental.pallas import tpu as pltpu
from jax.sharding import PartitionSpec as P

F32, BF16, I32 = jnp.float32, jnp.bfloat16, jnp.int32
ROOM = 12 * 1024 * 1024


def iota(shape, dim):
    return lax.broadcasted_iota(I32, shape, dim)


def call(kernel, outs, *args, hbm=(), scratch=(), order=None):
    if order is not None:
        inner, place = kernel, [order.index(i) for i in range(len(args))]

        def kernel(*refs):
            inner(*[refs[i] for i in place], *refs[len(place) :])

        args = [args[i] for i in order]
    spaces = [pltpu.HBM if i in hbm else pltpu.VMEM for i in range(len(args))]
    specs = [pl.BlockSpec(memory_space=m) for m in spaces]
    ops = [pltpu.with_memory_space_constraint(a, m) for a, m in zip(args, spaces)]
    held = sum(math.prod(m.shape) * jnp.dtype(m.dtype).itemsize for m in scratch if m.memory_space == pltpu.VMEM)
    return pl.pallas_call(
        kernel,
        out_shape=outs,
        in_specs=specs,
        out_specs=[pl.BlockSpec(memory_space=pltpu.VMEM)] * len(outs),
        scratch_shapes=list(scratch),
        cost_estimate=pl.CostEstimate(flops=1, bytes_accessed=1, transcendentals=0),
        compiler_params=pltpu.CompilerParams(vmem_limit_bytes=held + ROOM),
    )(*ops)


def tdot(a, b):
    return lax.dot_general(a, b, (((0,), (0,)), ((), ())), preferred_element_type=F32)


def dot(a, b):
    return jnp.dot(a, b, preferred_element_type=F32)


def where_am_i(ny, nk):
    r, c = lax.axis_index("row"), lax.axis_index("col")
    return r // ny, r % ny, c, c // nk, c % nk


def packed(row, fine, wide):
    block = row // fine
    return (1 + block // wide) * fine + row % fine, block % wide * fine


def prep_kernel(
    u_hbm, signs_hbm, weights_hbm, comp_hbm,
    probes, own, give1, give2, diag, scale,
    u, signs, weights, comp, raw, sems,
    *, nz, ny, nk, fine, rows,
):
    z, y, c, _, _ = where_am_i(ny, nk)
    ntiles = nz * ny
    take = 256 // ntiles
    parts = rows // (2 * take)
    wide = probes.shape[1] // fine
    pairs = [(signs_hbm, signs), (weights_hbm, weights), (u_hbm, u), (comp_hbm, comp)]
    gets = [pltpu.make_async_copy(a, b, sems.at[n]) for n, (a, b) in enumerate(pairs)]
    for g in gets:
        g.start()
    j, m = iota((256, 256), 0), iota((256, 256), 1)
    slot, i = j // take, j % take
    d = slot % nz
    side = jnp.where(slot < nz, y, 1 - y)
    tile = ((z + d) % nz) * ny + side
    pick = jnp.where(m == i * ntiles + tile, 1.0, 0.0).astype(BF16)
    eye = iota((fine, fine), 0) == iota((fine, fine), 1)
    gets[0].wait()
    gets[1].wait()
    wcol = jnp.sum(jnp.where(eye, weights[...], 0.0), axis=1, keepdims=True)
    pv = ((2 * signs[...] - 1).astype(F32) * wcol).astype(BF16)
    probes[...] = pv
    give1[0:fine, :] = pv
    gets[3].wait()
    scale[0:1, :] = jnp.broadcast_to(comp[0:1, 0:1], (1, fine))
    scale[1:2, :] = jnp.broadcast_to(comp[0:1, 1:2], (1, fine))
    gets[2].wait()
    for h in range(parts):
        x = jnp.concatenate([u[h * 512 : h * 512 + 256, :], u[h * 512 + 256 : h * 512 + 512, :]], axis=1)
        o = dot(pick, x)
        for g in range(2):
            r0 = h * 2 * take + g * take
            og = o[:, g * fine : (g + 1) * fine]
            for s in range(nz):
                part = og[s * take : (s + 1) * take]
                mirror = og[(nz + s) * take : (nz + s + 1) * take]
                if s == 0:
                    col = c * fine + iota((take, fine), 1)
                    row = r0 + iota((take, fine), 0)
                    raw[r0 : r0 + take, :] = part
                    own[r0 : r0 + take, 0:fine] = jnp.where(col > row, part, 0.0).astype(BF16)
                    own[r0 : r0 + take, nz * fine : (nz + 1) * fine] = jnp.where(y == 0, mirror, 0.0).astype(BF16)
                else:
                    own[r0 : r0 + take, s * fine : (s + 1) * fine] = part.astype(BF16)
                    if s > 1:
                        give2[r0 : r0 + take, (s - 2) * fine : (s - 1) * fine] = mirror.astype(BF16)
                    else:
                        top, left = packed(r0, fine, wide)
                        give1[top : top + take, left : left + fine] = mirror.astype(BF16)
    blk = raw[pl.ds(pl.multiple_of(c * fine, fine), fine), :]
    diag[...] = jnp.broadcast_to(jnp.sum(jnp.where(eye, blk, 0.0), axis=1, keepdims=True), (fine, fine))


def relay_kernel(*refs):
    out = refs[-1]
    out[...] = refs[0][0 : out.shape[0], :]


def stack_kernel(*refs, order):
    for i, r in zip(order, refs[:-1]):
        refs[-1][i] = r[0 : refs[-1].shape[1], :]


def direct_kernel(own, oth1, oth2, *refs, nz, ny, nx, nk, fine):
    ps, (keep, send, oth, p, d) = refs[: nz + 1], refs[nz + 1 :]
    _, _, _, x, k = where_am_i(ny, nk)
    for n in range(nz + 1):
        p[n * fine : (n + 1) * fine, :] = ps[n][0:fine, :]
    d[0] = dot(own[...], p[...])
    for r0 in range(0, oth.shape[0], fine):
        top, left = packed(r0, fine, p.shape[1] // fine)
        oth[r0 : r0 + fine, 0:fine] = oth1[top : top + fine, left : left + fine]
    oth[:, fine:] = oth2[...]
    d[1] = dot(oth[...], p[fine : nz * fine, :])
    for s in range(ny):
        for e in range(nx):
            xx = (x + e) % nx
            i = s * nx + e
            keep[i] = d[s, pl.ds(pl.multiple_of((xx * nk + k) * fine, fine), fine), :]
            send[i] = d[s, pl.ds(pl.multiple_of((xx * nk + 1 - k) * fine, fine), fine), :].astype(BF16)


def mirror_kernel(near, far, keep, own, oth, m0, mx, *refs, nz, ny, nx, nk, fine):
    ms, q = refs[:-1], refs[-1]
    _, _, _, x, k = where_am_i(ny, nk)
    for s in range(ny):
        for e in range(nx):
            xx = (x + e) % nx
            i = s * nx + e
            q[s, pl.ds(pl.multiple_of((xx * nk + k) * fine, fine), fine), :] = near[i]
            q[s, pl.ds(pl.multiple_of((xx * nk + 1 - k) * fine, fine), fine), :] = far[i]
    q0, q1 = q[0], q[1]
    mo = tdot(own[...], q0)
    m0[...] = mo[:fine]
    mx[...] = mo[nz * fine :]
    md = (mo[fine : nz * fine] + tdot(oth[...], q1)).astype(BF16)
    for d in range(1, nz):
        ms[d - 1][...] = md[(d - 1) * fine : d * fine]


def fold_kernel(keep, got, mx, *refs, nx, ny):
    n = (len(refs) - nx * ny) // 2
    held, home, pieces, passed = refs[:n], refs[n], refs[n + 1 : n + nx * ny], refs[n + nx * ny :]
    home[...] = keep[0] + got[0].astype(F32)
    for i in range(1, nx * ny):
        total = keep[i] + got[i].astype(F32)
        if i == nx:
            total = total + mx[...]
        pieces[i - 1][...] = total.astype(BF16)
    for a, b in zip(held, passed):
        b[...] = a[...]


def last_kernel(scale, probes, diag, *refs):
    out = refs[-1]
    total = refs[0][...].astype(F32)
    for r in refs[1:-1]:
        total = total + r[...].astype(F32)
    pf = probes[...].astype(F32)
    total = total + diag[:, 0:1] * pf
    out[...] = scale[0:1, 0:1] * total + scale[1:2, 0:1] * pf


def solution(mesh):
    nrow, ncol = mesh.shape["row"], mesh.shape["col"]
    ny, nk = 2, 2
    nz, nx = nrow // ny, ncol // nk
    both = ("row", "col")

    def place(z, y, x, k):
        return ((z * ny + y) * nx + x) * nk + k

    spots = [(z, y, x, k) for z in range(nz) for y in range(ny) for x in range(nx) for k in range(nk)]

    def down(d):
        return [(place(z, y, x, k), place(z - d, y, x, k)) for z, y, x, k in spots if z >= d]

    def up(d):
        return [(place(z, y, x, k), place(z + d, y, x, k)) for z, y, x, k in spots if z + d < nz]

    def hop(*steps):
        return [(place(a, y, x, k), place(b, y, x, k)) for a, b in steps for z, y, x, k in spots if z == 0]

    def shift(s, e):
        return [(place(z, y, x, k), place(z, y ^ s, (x + e) % nx, k)) for z, y, x, k in spots]

    other_core = [(place(z, y, x, k), place(z, y, x, 1 - k)) for z, y, x, k in spots]
    away = [(s, e) for s in range(ny) for e in range(nx) if (s, e) != (0, 0)]

    def body(upper, signs, weights, components):
        rows, ntiles, _, fine = upper.shape
        npro = signs.shape[1]
        blk = (fine, npro)
        nblk = nx * ny

        probes, own, give1, give2, diag, scale = call(
            functools.partial(prep_kernel, nz=nz, ny=ny, nk=nk, fine=fine, rows=rows),
            [
                pltpu.VMEM(blk, BF16),
                pltpu.VMEM((rows, (nz + 1) * fine), BF16),
                pltpu.VMEM((fine + rows * fine // npro, npro), BF16),
                pltpu.VMEM((rows, (nz - 2) * fine), BF16),
                pltpu.VMEM((fine, fine), F32),
                pltpu.VMEM((2, fine), F32),
            ],
            upper.reshape(rows * ntiles, fine), signs, weights.reshape(1, fine), components.reshape(1, 2),
            hbm=(0, 1, 2, 3),
            scratch=[
                pltpu.VMEM((rows * ntiles, fine), BF16),
                pltpu.VMEM(blk, I32),
                pltpu.VMEM((1, fine), F32),
                pltpu.VMEM((1, 2), F32),
                pltpu.VMEM((rows, fine), F32),
                pltpu.SemaphoreType.DMA((4,)),
            ],
        )
        oth1 = lax.ppermute(give1, both, shift(1, 0))
        downs = {1: lax.ppermute(probes, both, down(1))}
        pairs = [(a, b) for a, b in shift(1, 0) if a // (ny * nx * nk) < nz - 2]
        oth2 = lax.ppermute(give2, both, pairs)
        if nz == 4:
            downs[3] = lax.ppermute(probes, both, down(3))
        near = {(0, 0): probes}
        for e in range(1, nx):
            near[0, e] = lax.ppermute(probes, both, shift(0, nx - e))
        have = {"a": downs[1], "x": near[0, 1], "y": oth1, "b": downs.get(3, downs[1])}
        (pad,) = call(
            relay_kernel, [pltpu.VMEM(blk, BF16)], oth1
        )
        near[1, 0] = pad
        for e in range(1, nx):
            near[1, e] = lax.ppermute(pad, both, shift(0, nx - e))
        if nz == 4:
            handed = downs[1]
            if 'xyb':
                (handed,) = call(relay_kernel, [pltpu.VMEM(blk, BF16)], handed, *[have[n] for n in 'yb'])
            downs[2] = lax.ppermute(handed, both, hop((2, 1), (1, 0)))
        else:
            downs |= {d: lax.ppermute(probes, both, down(d)) for d in range(2, nz)}
        order = [(s, e) for s in range(ny) for e in range(nx)]
        if nz == 4:
            order = [order[i] for i in [2, 0, 1, 3]]
        (stack,) = call(
            functools.partial(stack_kernel, order=[s * nx + e for s, e in order]),
            [pltpu.VMEM((nblk, *blk), BF16)],
            *[near[p] for p in order],
        )
        far = lax.ppermute(stack, both, other_core)
        oth2, downs = lax.optimization_barrier((oth2, downs))
        keep, send, oth = call(
            functools.partial(direct_kernel, nz=nz, ny=ny, nx=nx, nk=nk, fine=fine),
            [pltpu.VMEM((nblk, *blk), F32), pltpu.VMEM((nblk, *blk), BF16), pltpu.VMEM((rows, (nz - 1) * fine), BF16)],
            own, oth1, oth2, probes, *[downs[d] for d in range(1, nz)], near[1, 0],
            scratch=[pltpu.VMEM(((nz + 1) * fine, npro), BF16), pltpu.VMEM((ny, rows, npro), F32)],
            order=[0, 1, 2, 3, 4, 5, 6, 7] if nz == 4 else None,
        )
        got = lax.ppermute(send, both, other_core)
        m0, mx, *ms = call(
            functools.partial(mirror_kernel, nz=nz, ny=ny, nx=nx, nk=nk, fine=fine),
            [pltpu.VMEM(blk, F32), pltpu.VMEM(blk, F32)] + [pltpu.VMEM(blk, BF16)] * (nz - 1),
            stack, far, keep, own, oth,
            scratch=[pltpu.VMEM((ny, rows, npro), BF16)],
            order=[0, 1, 2, 3, 4] if nz == 4 else None,
        )
        steps = [1, 2, 3] if nz == 4 else list(range(1, nz))
        direct, chain = (1, 1) if nz == 4 else (1, False)
        climbs = [[(z, z + d) for z in range(nz - d)] for d in steps]
        ups = [lax.ppermute(ms[d - 1], both, hop(*climbs[i])) for i, d in enumerate(steps) if i < direct]
        home, *rest = call(
            functools.partial(fold_kernel, nx=nx, ny=ny),
            [pltpu.VMEM(blk, F32)] + [pltpu.VMEM(blk, BF16)] * (nblk - 1 + nz - 1 - direct),
            keep, got, mx, *[ms[d - 1] for d in steps[direct:]],
        )
        pieces, held = rest[: nblk - 1], rest[nblk - 1 :]
        cross = [lax.ppermute(p, both, shift(s, e)) for p, (s, e) in zip(pieces, away)]
        for n, h in enumerate(held):
            if chain and n == len(held) - 1:
                (h,) = call(relay_kernel, [pltpu.VMEM(blk, BF16)], h, ups[0])
            ups.append(lax.ppermute(h, both, hop(*climbs[direct + n])))
        tail = [scale, probes, diag, m0, home, *ups, *cross]
        (out,) = call(
            last_kernel, [jax.ShapeDtypeStruct(blk, F32)], *tail,
            order=[4, 1, 0, 5, 7, 2, 10, 6, 3, 8, 9] if nz == 4 else None,
        )
        return out

    return jax.shard_map(
        body,
        mesh=mesh,
        in_specs=(P("row", None, "col", None), P(both, None), P(both), P()),
        out_specs=P(both, None),
        check_vma=False,
    )
```

```python
import functools
import math

import jax
import jax.numpy as jnp
from jax import lax
from jax.experimental import pallas as pl
from jax.experimental.pallas import tpu as pltpu
from jax.sharding import PartitionSpec as P

F32, BF16, I32 = jnp.float32, jnp.bfloat16, jnp.int32
ROOM = 12 * 1024 * 1024


def iota(shape, dim):
    return lax.broadcasted_iota(I32, shape, dim)


def call(kernel, outs, *args, hbm=(), scratch=(), order=None, to=pltpu.VMEM):
    if order is not None:
        inner, place = kernel, [order.index(i) for i in range(len(args))]

        def kernel(*refs):
            inner(*[refs[i] for i in place], *refs[len(place) :])

        args = [args[i] for i in order]
    spaces = [pltpu.HBM if i in hbm else pltpu.VMEM for i in range(len(args))]
    specs = [pl.BlockSpec(memory_space=m) for m in spaces]
    ops = [pltpu.with_memory_space_constraint(a, m) for a, m in zip(args, spaces)]
    held = sum(math.prod(m.shape) * jnp.dtype(m.dtype).itemsize for m in scratch if m.memory_space == pltpu.VMEM)
    return pl.pallas_call(
        kernel,
        out_shape=outs,
        in_specs=specs,
        out_specs=[pl.BlockSpec(memory_space=to)] * len(outs),
        scratch_shapes=list(scratch),
        cost_estimate=pl.CostEstimate(flops=1, bytes_accessed=1, transcendentals=0),
        compiler_params=pltpu.CompilerParams(vmem_limit_bytes=held + ROOM),
    )(*ops)


def tdot(a, b):
    return lax.dot_general(a, b, (((0,), (0,)), ((), ())), preferred_element_type=F32)


def dot(a, b):
    return jnp.dot(a, b, preferred_element_type=F32)


def where_am_i(ny, nk):
    r, c = lax.axis_index("row"), lax.axis_index("col")
    return r // ny, r % ny, c, c // nk, c % nk


def packed(row, fine, wide):
    block = row // fine
    return (1 + block // wide) * fine + row % fine, block % wide * fine


def prep_kernel(
    u_hbm, signs_hbm, weights_hbm, comp_hbm,
    probes, own, give1, give2, diag, scale,
    u, signs, weights, comp, raw, sems,
    *, nz, ny, nk, fine, rows,
):
    z, y, c, _, _ = where_am_i(ny, nk)
    ntiles = nz * ny
    take = 256 // ntiles
    parts = rows // (2 * take)
    wide = probes.shape[1] // fine
    pairs = [(signs_hbm, signs), (weights_hbm, weights), (u_hbm, u), (comp_hbm, comp)]
    gets = [pltpu.make_async_copy(a, b, sems.at[n]) for n, (a, b) in enumerate(pairs)]
    for g in gets:
        g.start()
    j, m = iota((256, 256), 0), iota((256, 256), 1)
    slot, i = j // take, j % take
    d = slot % nz
    side = jnp.where(slot < nz, y, 1 - y)
    tile = ((z + d) % nz) * ny + side
    pick = jnp.where(m == i * ntiles + tile, 1.0, 0.0).astype(BF16)
    eye = iota((fine, fine), 0) == iota((fine, fine), 1)
    gets[0].wait()
    gets[1].wait()
    wcol = jnp.sum(jnp.where(eye, weights[...], 0.0), axis=1, keepdims=True)
    pv = ((2 * signs[...] - 1).astype(F32) * wcol).astype(BF16)
    probes[...] = pv
    give1[0:fine, :] = pv
    gets[3].wait()
    scale[0:1, :] = jnp.broadcast_to(comp[0:1, 0:1], (1, fine))
    scale[1:2, :] = jnp.broadcast_to(comp[0:1, 1:2], (1, fine))
    gets[2].wait()
    for h in range(parts):
        x = jnp.concatenate([u[h * 512 : h * 512 + 256, :], u[h * 512 + 256 : h * 512 + 512, :]], axis=1)
        o = dot(pick, x)
        for g in range(2):
            r0 = h * 2 * take + g * take
            og = o[:, g * fine : (g + 1) * fine]
            for s in range(nz):
                part = og[s * take : (s + 1) * take]
                mirror = og[(nz + s) * take : (nz + s + 1) * take]
                if s == 0:
                    col = c * fine + iota((take, fine), 1)
                    row = r0 + iota((take, fine), 0)
                    raw[r0 : r0 + take, :] = part
                    own[r0 : r0 + take, 0:fine] = jnp.where(col > row, part, 0.0).astype(BF16)
                    own[r0 : r0 + take, nz * fine : (nz + 1) * fine] = jnp.where(y == 0, mirror, 0.0).astype(BF16)
                else:
                    own[r0 : r0 + take, s * fine : (s + 1) * fine] = part.astype(BF16)
                    if s > 1:
                        give2[r0 : r0 + take, (s - 2) * fine : (s - 1) * fine] = mirror.astype(BF16)
                    else:
                        top, left = packed(r0, fine, wide)
                        give1[top : top + take, left : left + fine] = mirror.astype(BF16)
    blk = raw[pl.ds(pl.multiple_of(c * fine, fine), fine), :]
    diag[...] = jnp.broadcast_to(jnp.sum(jnp.where(eye, blk, 0.0), axis=1, keepdims=True), (fine, fine))


def relay_kernel(*refs):
    out = refs[-1]
    out[...] = refs[0][0 : out.shape[0], :]


def stack_kernel(*refs, order):
    for i, r in zip(order, refs[:-1]):
        refs[-1][i] = r[0 : refs[-1].shape[1], :]


def direct_kernel(own, oth1, oth2, *refs, nz, ny, nx, nk, fine):
    ps, (keep, send, oth, p, d) = refs[: nz + 1], refs[nz + 1 :]
    _, _, _, x, k = where_am_i(ny, nk)
    for n in range(nz + 1):
        p[n * fine : (n + 1) * fine, :] = ps[n][0:fine, :]
    d[0] = dot(own[...], p[...])
    for r0 in range(0, oth.shape[0], fine):
        top, left = packed(r0, fine, p.shape[1] // fine)
        oth[r0 : r0 + fine, 0:fine] = oth1[top : top + fine, left : left + fine]
    oth[:, fine:] = oth2[...]
    d[1] = dot(oth[...], p[fine : nz * fine, :])
    for s in range(ny):
        for e in range(nx):
            xx = (x + e) % nx
            i = s * nx + e
            keep[i] = d[s, pl.ds(pl.multiple_of((xx * nk + k) * fine, fine), fine), :]
            send[i] = d[s, pl.ds(pl.multiple_of((xx * nk + 1 - k) * fine, fine), fine), :].astype(BF16)


def mirror_kernel(near, far, keep, own, oth, m0, mx, *refs, nz, ny, nx, nk, fine):
    ms, q = refs[:-1], refs[-1]
    _, _, _, x, k = where_am_i(ny, nk)
    for s in range(ny):
        for e in range(nx):
            xx = (x + e) % nx
            i = s * nx + e
            q[s, pl.ds(pl.multiple_of((xx * nk + k) * fine, fine), fine), :] = near[i]
            q[s, pl.ds(pl.multiple_of((xx * nk + 1 - k) * fine, fine), fine), :] = far[i]
    q0, q1 = q[0], q[1]
    mo = tdot(own[...], q0)
    m0[...] = mo[:fine]
    mx[...] = mo[nz * fine :]
    md = (mo[fine : nz * fine] + tdot(oth[...], q1)).astype(BF16)
    for d in range(1, nz):
        ms[d - 1][...] = md[(d - 1) * fine : d * fine]


def fold_kernel(keep, got, mx, *refs, nx, ny):
    n = (len(refs) - nx * ny) // 2
    held, home, pieces, passed = refs[:n], refs[n], refs[n + 1 : n + nx * ny], refs[n + nx * ny :]
    home[...] = keep[0] + got[0].astype(F32)
    for i in range(1, nx * ny):
        total = keep[i] + got[i].astype(F32)
        if i == nx:
            total = total + mx[...]
        pieces[i - 1][...] = total.astype(BF16)
    for a, b in zip(held, passed):
        b[...] = a[...]


def last_kernel(scale, probes, diag, *refs):
    out, hold, sems = refs[-3:]
    step = hold.shape[0] // 4
    puts = []
    for n in range(4):
        at = pl.ds(n * step, step)
        total = refs[0][at, :].astype(F32)
        for r in refs[1:-3]:
            total = total + r[at, :].astype(F32)
        pf = probes[at, :].astype(F32)
        total = total + diag[at, 0:1] * pf
        hold[at, :] = scale[0:1, 0:1] * total + scale[1:2, 0:1] * pf
        puts.append(pltpu.make_async_copy(hold.at[at, :], out.at[at, :], sems.at[n]))
        puts[n].start()
    for p in puts:
        p.wait()


def solution(mesh):
    nrow, ncol = mesh.shape["row"], mesh.shape["col"]
    ny, nk = 2, 2
    nz, nx = nrow // ny, ncol // nk
    both = ("row", "col")

    def place(z, y, x, k):
        return ((z * ny + y) * nx + x) * nk + k

    spots = [(z, y, x, k) for z in range(nz) for y in range(ny) for x in range(nx) for k in range(nk)]

    def down(d):
        return [(place(z, y, x, k), place(z - d, y, x, k)) for z, y, x, k in spots if z >= d]

    def up(d):
        return [(place(z, y, x, k), place(z + d, y, x, k)) for z, y, x, k in spots if z + d < nz]

    def hop(*steps):
        return [(place(a, y, x, k), place(b, y, x, k)) for a, b in steps for z, y, x, k in spots if z == 0]

    def shift(s, e):
        return [(place(z, y, x, k), place(z, y ^ s, (x + e) % nx, k)) for z, y, x, k in spots]

    other_core = [(place(z, y, x, k), place(z, y, x, 1 - k)) for z, y, x, k in spots]
    away = [(s, e) for s in range(ny) for e in range(nx) if (s, e) != (0, 0)]

    def body(upper, signs, weights, components):
        rows, ntiles, _, fine = upper.shape
        npro = signs.shape[1]
        blk = (fine, npro)
        nblk = nx * ny

        probes, own, give1, give2, diag, scale = call(
            functools.partial(prep_kernel, nz=nz, ny=ny, nk=nk, fine=fine, rows=rows),
            [
                pltpu.VMEM(blk, BF16),
                pltpu.VMEM((rows, (nz + 1) * fine), BF16),
                pltpu.VMEM((fine + rows * fine // npro, npro), BF16),
                pltpu.VMEM((rows, (nz - 2) * fine), BF16),
                pltpu.VMEM((fine, fine), F32),
                pltpu.VMEM((2, fine), F32),
            ],
            upper.reshape(rows * ntiles, fine), signs, weights.reshape(1, fine), components.reshape(1, 2),
            hbm=(0, 1, 2, 3),
            scratch=[
                pltpu.VMEM((rows * ntiles, fine), BF16),
                pltpu.VMEM(blk, I32),
                pltpu.VMEM((1, fine), F32),
                pltpu.VMEM((1, 2), F32),
                pltpu.VMEM((rows, fine), F32),
                pltpu.SemaphoreType.DMA((4,)),
            ],
        )
        oth1 = lax.ppermute(give1, both, shift(1, 0))
        downs = {1: lax.ppermute(probes, both, down(1))}
        pairs = [(a, b) for a, b in shift(1, 0) if a // (ny * nx * nk) < nz - 2]
        oth2 = lax.ppermute(give2, both, pairs)
        if nz == 4:
            downs[3] = lax.ppermute(probes, both, down(3))
        near = {(0, 0): probes}
        for e in range(1, nx):
            near[0, e] = lax.ppermute(probes, both, shift(0, nx - e))
        have = {"a": downs[1], "x": near[0, 1], "y": oth1, "b": downs.get(3, downs[1])}
        (pad,) = call(
            relay_kernel, [pltpu.VMEM(blk, BF16)], oth1
        )
        near[1, 0] = pad
        for e in range(1, nx):
            near[1, e] = lax.ppermute(pad, both, shift(0, nx - e))
        if nz == 4:
            handed = downs[1]
            if 'xyb':
                (handed,) = call(relay_kernel, [pltpu.VMEM(blk, BF16)], handed, *[have[n] for n in 'yb'])
            downs[2] = lax.ppermute(handed, both, hop((2, 1), (1, 0)))
        else:
            downs |= {d: lax.ppermute(probes, both, down(d)) for d in range(2, nz)}
        order = [(s, e) for s in range(ny) for e in range(nx)]
        if nz == 4:
            order = [order[i] for i in [2, 0, 1, 3]]
        (stack,) = call(
            functools.partial(stack_kernel, order=[s * nx + e for s, e in order]),
            [pltpu.VMEM((nblk, *blk), BF16)],
            *[near[p] for p in order],
        )
        far = lax.ppermute(stack, both, other_core)
        oth2, downs = lax.optimization_barrier((oth2, downs))
        keep, send, oth = call(
            functools.partial(direct_kernel, nz=nz, ny=ny, nx=nx, nk=nk, fine=fine),
            [pltpu.VMEM((nblk, *blk), F32), pltpu.VMEM((nblk, *blk), BF16), pltpu.VMEM((rows, (nz - 1) * fine), BF16)],
            own, oth1, oth2, probes, *[downs[d] for d in range(1, nz)], near[1, 0],
            scratch=[pltpu.VMEM(((nz + 1) * fine, npro), BF16), pltpu.VMEM((ny, rows, npro), F32)],
            order=[0, 1, 2, 3, 4, 5, 6, 7] if nz == 4 else None,
        )
        got = lax.ppermute(send, both, other_core)
        m0, mx, *ms = call(
            functools.partial(mirror_kernel, nz=nz, ny=ny, nx=nx, nk=nk, fine=fine),
            [pltpu.VMEM(blk, F32), pltpu.VMEM(blk, F32)] + [pltpu.VMEM(blk, BF16)] * (nz - 1),
            stack, far, keep, own, oth,
            scratch=[pltpu.VMEM((ny, rows, npro), BF16)],
            order=[0, 1, 2, 3, 4] if nz == 4 else None,
        )
        steps = [1, 2, 3] if nz == 4 else list(range(1, nz))
        direct, chain = (2, 1) if nz == 4 else (1, False)
        climbs = [[(z, z + d) for z in range(nz - d)] for d in steps]
        ups = [lax.ppermute(ms[d - 1], both, hop(*climbs[i])) for i, d in enumerate(steps) if i < direct]
        home, *rest = call(
            functools.partial(fold_kernel, nx=nx, ny=ny),
            [pltpu.VMEM(blk, F32)] + [pltpu.VMEM(blk, BF16)] * (nblk - 1 + nz - 1 - direct),
            keep, got, mx, *[ms[d - 1] for d in steps[direct:]],
        )
        pieces, held = rest[: nblk - 1], rest[nblk - 1 :]
        cross = [lax.ppermute(p, both, shift(s, e)) for p, (s, e) in zip(pieces, away)]
        for n, h in enumerate(held):
            if chain and n == len(held) - 1:
                (h,) = call(relay_kernel, [pltpu.VMEM(blk, BF16)], h, ups[0])
            ups.append(lax.ppermute(h, both, hop(*climbs[direct + n])))
        tail = [scale, probes, diag, m0, home, *ups, *cross]
        (out,) = call(
            last_kernel, [jax.ShapeDtypeStruct(blk, F32)], *tail, to=pl.ANY,
            scratch=[pltpu.VMEM(blk, F32), pltpu.SemaphoreType.DMA((4,))],
            order=[4, 1, 0, 5, 7, 2, 10, 6, 3, 8, 9] if nz == 4 else None,
        )
        return out

    return jax.shard_map(
        body,
        mesh=mesh,
        in_specs=(P("row", None, "col", None), P(both, None), P(both), P()),
        out_specs=P(both, None),
        check_vma=False,
    )
```
